128 devices in a mesh: dp: 8 (over y_hi, x), mp: 16 (over z, y_lo, core).
Axes of the slice: x: 4, y: 4 (y_hi: 2, y_lo: 2; y = y_hi * 2 + y_lo), z: 4, core: 2. Of those that a mesh axis runs over, the one named last changes fastest.
Arguments:
- tokens: bfloat16 [6144, 16384], P('dp', 'mp'), may hold values from -6 to 6
- cotangent: bfloat16 [6144, 16384], P('dp', 'mp'), may hold values from -6 to 6
- blocks_w: bfloat16 [16, 5, 1024, 1024], P('mp'), may hold values from -0.078125 to 0.078125
- lowrank_u: bfloat16 [16384, 256], P('mp'), may hold values from -0.046875 to 0.046875
- lowrank_v: bfloat16 [256, 16384], P(None, 'mp'), may hold values from -0.375 to 0.375
Outputs:
- grad_tokens: float32 [6144, 16384], P('dp', 'mp')
- grad_blocks: float32 [1024, 16, 5, 1024], P('dp', 'mp')
- grad_u: float32 [16384, 256], P(('mp', 'dp'))
- grad_v: float32 [256, 16384], P(None, ('mp', 'dp'))
The draws below stay inside these ranges and needn't reach their ends.
All inputs are finite; a program needn't handle non-finite values.
Results may differ from the reference program's by a relative error of at most 0.0029.
Values may be sent and summed in bfloat16 or wider, within the bound.
A program may use at most 192 MiB of HBM per device.

```python
import math
import jax
import jax.numpy as jnp
from jax import lax

NB = 16
BLK = 1024
R = 256
TOK_DEV = 768
SLOTS = 5
D = 16384
TOKENS = 6144
N_DP = 8


def level_of(own_key, dims, cuts, smallest, high):
    gain, own = 1.0, jax.random.fold_in(own_key, 6)
    for axis_at, parts in cuts:
        heights = jnp.exp(jax.random.uniform(jax.random.fold_in(own, axis_at), (parts,), jnp.float32, smallest / len(cuts), high / len(cuts)))
        gain = gain * jnp.repeat(heights, dims[axis_at] // parts).reshape([-1 if axis == axis_at else 1 for axis in range(len(dims))])
    return gain


def bell_draw(own_key, extent, deviation, most, pieces=(), kind=jnp.bfloat16):
    array = jax.random.normal(own_key, extent, jnp.float32) * deviation
    if len(pieces) > 0:
        array = level_of(own_key, extent, pieces, -0.22, 0.18) * array
    return jnp.clip(array, min=-most, max=most).astype(kind)


def setup_inputs(seed: int = 0) -> dict:
    key_of = jax.random.split(jax.random.key(seed), 6)
    tokens = bell_draw(key_of[0], (TOKENS, D), 1.0, 6.0, ((0, 8), (1, 16)))
    cotangent = bell_draw(key_of[1], (TOKENS, D), 1.0, 6.0, ((0, 8), (1, 16)))
    blocks_w = bell_draw(key_of[2], (NB, SLOTS, BLK, BLK), (SLOTS * BLK) ** -0.5, 0.078125, ((0, 16),))
    lowrank_u = bell_draw(key_of[3], (D, R), D ** -0.5, 0.046875, ((0, 16),))
    lowrank_v = bell_draw(key_of[4], (R, D), R ** -0.5, 0.375, ((1, 16),))
    return {"tokens": tokens, "cotangent": cotangent, "blocks_w": blocks_w, "lowrank_u": lowrank_u, "lowrank_v": lowrank_v}


def source_block(block, slot):
    if slot == 0:
        return block
    return block ^ 1 << slot - 1

def reference(tokens, cotangent, blocks_w, lowrank_u, lowrank_v):
    grad_scale = 1.0 / math.sqrt(TOKENS)
    tok_blocks = tokens.reshape(TOKENS, NB, BLK)
    cot_blocks = cotangent.reshape(TOKENS, NB, BLK)
    low_in = jnp.dot(tokens, lowrank_u, preferred_element_type=jnp.float32).astype(jnp.bfloat16)
    low_back = jnp.dot(cotangent, lowrank_v.T, preferred_element_type=jnp.float32).astype(jnp.bfloat16)
    back_low = jnp.dot(low_back, lowrank_u.T, preferred_element_type=jnp.float32)
    columns = []
    for block in range(NB):
        total = back_low[:, block * BLK:(block + 1) * BLK]
        for slot in range(SLOTS):
            other = source_block(block, slot)
            total = total + jnp.dot(cot_blocks[:, other], blocks_w[other, slot].T, preferred_element_type=jnp.float32)
        columns.append(total)
    grad_tokens = jnp.concatenate(columns, axis=1)
    grads = []
    for block in range(NB):
        cot_shards = cot_blocks[:, block].reshape(N_DP, TOK_DEV, BLK).astype(jnp.float32)
        slot_grads = []
        for slot in range(SLOTS):
            tok_shards = tok_blocks[:, source_block(block, slot)].reshape(N_DP, TOK_DEV, BLK).astype(jnp.float32)
            partial_value = jnp.einsum('nti,nto->nio', tok_shards, cot_shards)
            slot_grads.append(lax.optimization_barrier(jnp.sum(partial_value, axis=0)) * grad_scale)
        grads.append(jnp.stack(slot_grads, axis=1))
    grad_blocks = jnp.stack(grads, axis=1)
    grad_u = jnp.dot(tokens.T, low_back, preferred_element_type=jnp.float32) * grad_scale
    grad_v = jnp.dot(low_in.T, cotangent, preferred_element_type=jnp.float32) * grad_scale
    return (grad_tokens, grad_blocks, grad_u, grad_v)
```

```python
import functools
import math

import jax
import jax.numpy as jnp
from jax import lax
from jax.experimental import pallas as pl
from jax.experimental.pallas import tpu as pltpu
from jax.sharding import PartitionSpec as P

MESH = pl.DeviceIdType.MESH
F32 = jnp.float32
BF16 = jnp.bfloat16
CHUNKS = 4


def flip(value, bit):
    return value + bit - 2 * bit * lax.rem(lax.div(value, bit), 2)


def dot_nt(a, b):
    return lax.dot_general(a, b, (((1,), (1,)), ((), ())), preferred_element_type=F32)


def dot_tn(a, b):
    return lax.dot_general(a, b, (((0,), (0,)), ((), ())), preferred_element_type=F32)


def kernel(
    rows, blk, rank, scale,
    tok_hbm, cot_hbm, w_hbm, u_hbm, v_hbm,
    gt_hbm, gb_hbm, gu_ref, gv_ref,
    tq, cx, tx, w, uu, vv,
    s4, s34, s2, s1, r4, r34, r2, r1,
    acc, ps, pr, gt,
    lp, lr1, lr2, lz, lr3, lf,
    eb, er, eo, eyu, eyv,
    lsem, ssem, rsem,
):
    qw = blk // 8
    dp = lax.axis_index("dp")
    mp = lax.axis_index("mp")
    x = lax.rem(dp, 4)
    yh = lax.div(dp, 4)
    core = lax.rem(mp, 2)
    z = lax.div(mp, 4)

    def px(rel):
        return (yh * 4 + lax.rem(x + rel, 4), mp)

    m1 = (dp, flip(mp, 1))
    m2 = (dp, flip(mp, 2))
    m4 = (dp, flip(mp, 4))
    m8 = (dp, flip(mp, 8))
    m12 = (dp, flip(flip(mp, 4), 8))
    yy = (flip(dp, 4), mp)

    nl = [0]

    def load(src, dst):
        cp = pltpu.make_async_copy(src, dst, lsem.at[nl[0]])
        nl[0] += 1
        cp.start()
        return cp

    own = []
    tl = []
    for h in range(2):
        own.append(load(
            tok_hbm.at[:, pl.ds(pl.multiple_of(h * 4 * qw + x * qw, qw), qw)],
            tx.at[0, 0, :, pl.ds(h * qw, qw)],
        ))
    for q in range(4):
        for h in range(2):
            tl.append(load(
                tok_hbm.at[:, pl.ds(h * 4 * qw + q * qw, qw)],
                tq.at[q, :, pl.ds(h * qw, qw)],
            ))
    cl = load(cot_hbm, cx.at[0])
    ul = load(u_hbm, uu)
    vl = load(v_hbm, vv)
    wl = {s: load(w_hbm.at[s], w.at[s]) for s in (4, 3, 2, 1, 0)}

    barrier = pltpu.get_barrier_semaphore()
    peers = [px(1), px(3), px(2), m1, m2, m4, m8, m12, yy]
    for peer in peers:
        pl.semaphore_signal(barrier, 1, device_id=peer, device_id_type=MESH)
    pl.semaphore_wait(barrier, len(peers))

    ns = [0]
    sent = []

    def send(src, dst, peer):
        k = ns[0]
        ns[0] += 1
        cp = pltpu.make_async_remote_copy(
            src_ref=src, dst_ref=dst, send_sem=ssem.at[k], recv_sem=rsem.at[k],
            device_id=peer, device_id_type=MESH,
        )
        cp.start()
        sent.append(cp)
        return k, peer

    def recv(key, dst):
        k, peer = key
        pltpu.make_async_remote_copy(
            src_ref=dst, dst_ref=dst, send_sem=ssem.at[k], recv_sem=rsem.at[k],
            device_id=peer, device_id_type=MESH,
        ).wait_recv()

    for cp in tl:
        cp.wait()
    xt = {}
    for rel in (1, 3, 2):
        slot = (4 - rel) % 4
        xt[slot] = send(tq.at[lax.rem(x + rel, 4)], tx.at[0, slot], px(rel))
    for cp in own:
        cp.wait()
    tm = {}

    def spread(slot):
        tm[3, slot] = send(tx.at[0, slot], tx.at[3, slot], m4)
        tm[2, slot] = send(tx.at[0, slot], tx.at[2, slot], m2)
        tm[1, slot] = send(tx.at[0, slot], tx.at[1, slot], m1)

    def onward(slot):
        recv(tm[3, slot], tx.at[3, slot])
        tm[4, slot] = send(tx.at[3, slot], tx.at[4, slot], m12)

    spread(0)
    cl.wait()
    half = rows // 2
    lo, hi = pl.ds(0, half), pl.ds(half, half)
    xc = {}
    xc[3, 0] = send(cx.at[0, lo], cx.at[3, lo], px(1))
    xc[1, 1] = send(cx.at[0, hi], cx.at[1, hi], px(3))
    xc[3, 1] = send(cx.at[0, hi], cx.at[3, hi], px(1))
    xc[1, 0] = send(cx.at[0, lo], cx.at[1, lo], px(3))

    ul.wait()
    vl.wait()
    low = jnp.zeros((rows, rank), F32)
    for q in range(4):
        uq = jnp.concatenate(
            [uu[q * qw:(q + 1) * qw, :], uu[(4 + q) * qw:(5 + q) * qw, :]], axis=0
        )
        low = low + jnp.dot(tq[q], uq, preferred_element_type=F32)
    lp[:, 0:rank] = low
    lp[:, rank:2 * rank] = dot_nt(cx[0], vv[...])
    hr = rows // 2
    a1 = send(lp.at[pl.ds(pl.multiple_of((1 - core) * hr, hr), hr)], lr1, m1)

    tile = blk // 4

    def term(slot, out, first, count, extra=None):
        at = pl.ds(first, count)

        def step(n, carry):
            cols = pl.ds(pl.multiple_of(n * tile, tile), tile)
            value = dot_nt(cx[0, at, :], w[slot, cols, :])
            if extra is not None:
                value = value + extra[at, cols].astype(F32)
            out[at, cols] = value.astype(BF16)
            return carry

        lax.fori_loop(0, 4, step, 0)

    cr = rows // CHUNKS
    wl[4].wait()
    t4 = []
    for c in range(CHUNKS):
        term(4, s4, c * cr, cr)
        at = pl.ds(c * cr, cr)
        t4.append(send(s4.at[at], r4.at[at], m12))
        if c == 1:
            recv(a1, lr1)
            mine = pl.ds(pl.multiple_of(core * hr, hr), hr)
            lr1[...] = lr1[...] + lp[mine, :]
            zr = hr // 4
            a2 = {}
            for v, peer in ((1, m4), (3, m12), (2, m8)):
                zz = z
                if v & 1:
                    zz = flip(zz, 1)
                if v & 2:
                    zz = flip(zz, 2)
                a2[v] = send(
                    lr1.at[pl.ds(pl.multiple_of(zz * zr, zr), zr)], lr2.at[v - 1], peer
                )
    onward(0)
    for slot in (3, 1):
        recv(xt[slot], tx.at[0, slot])
        spread(slot)
    for v in (1, 3, 2):
        recv(a2[v], lr2.at[v - 1])
    lz[...] = (
        lr1[pl.ds(pl.multiple_of(z * zr, zr), zr), :] + lr2[0] + lr2[1] + lr2[2]
    )
    a3 = send(lz, lr3, m2)
    recv(xt[2], tx.at[0, 2])
    spread(2)
    wl[2].wait()
    term(2, s2, 0, rows)
    t2 = send(s2, r2, m2)
    wl[1].wait()
    term(1, s1, 0, rows)
    t1 = send(s1, r1, m1)
    onward(3)
    onward(1)
    recv(a3, lr3)
    piece = pl.ds(pl.multiple_of(core * hr + z * zr, zr), zr)
    lf[piece, :] = (lz[...] + lr3[...]).astype(BF16)
    a4 = {}
    for v, peer in ((1, m4), (3, m12), (2, m8)):
        a4[v] = send(lf.at[piece], lf.at[piece], peer)
    wl[3].wait()
    t34 = []

    def chain(c):
        at = pl.ds(c * cr, cr)
        recv(t4[c], r4.at[at])
        term(3, s34, c * cr, cr, r4)
        t34.append(send(s34.at[at], r34.at[at], m4))

    chain(0)
    chain(1)
    onward(2)
    recv(xc[3, 0], cx.at[3, lo])
    xf0 = send(cx.at[3, lo], cx.at[2, lo], px(1))
    recv(xc[1, 1], cx.at[1, hi])
    xf1 = send(cx.at[1, hi], cx.at[2, hi], px(3))
    chain(2)
    for v in (1, 3, 2):
        zz = z
        if v & 1:
            zz = flip(zz, 1)
        if v & 2:
            zz = flip(zz, 2)
        recv(a4[v], lf.at[pl.ds(pl.multiple_of(core * hr + zz * zr, zr), zr)])
    mine = pl.ds(pl.multiple_of(core * hr, hr), hr)
    other = pl.ds(pl.multiple_of((1 - core) * hr, hr), hr)
    a5 = send(lf.at[mine], lf.at[mine], m1)
    chain(3)

    wide = blk // 2

    def product(slot, first):
        def step(i, carry):
            s = lax.div(i, 2)
            cols = pl.ds(pl.multiple_of(lax.rem(i, 2) * wide, wide), wide)
            value = dot_tn(tx[s, slot], cx[slot, :, cols])
            if first:
                acc[s, :, cols] = value
            else:
                acc[s, :, cols] = acc[s, :, cols] + value
            return carry
        return step

    for s in (1, 2):
        recv(tm[s, 0], tx.at[s, 0])
    recv(tm[4, 0], tx.at[4, 0])
    lax.fori_loop(0, 10, product(0, True), 0)

    recv(a5, lf.at[other])
    ex = {}
    for rel in (1, 3, 2, 0):
        q = lax.rem(x + rel, 4)
        gu = dot_tn(tq[q], lf[:, rank:2 * rank])
        ga = dot_tn(lf[:, 0:rank], cx[0, :, pl.ds(pl.multiple_of(q * qw, qw), qw)])
        gb = dot_tn(lf[:, 0:rank], cx[0, :, pl.ds(pl.multiple_of(4 * qw + q * qw, qw), qw)])
        if rel == 0:
            eo[0:2 * qw, :] = gu
            eo[2 * qw:2 * qw + rank, 0:qw] = ga
            eo[2 * qw:2 * qw + rank, qw:2 * qw] = gb
        else:
            eb[rel - 1, 0:2 * qw, :] = gu.astype(BF16)
            eb[rel - 1, 2 * qw:2 * qw + rank, 0:qw] = ga.astype(BF16)
            eb[rel - 1, 2 * qw:2 * qw + rank, qw:2 * qw] = gb.astype(BF16)
            ex[rel] = send(eb.at[rel - 1], er.at[rel - 1], px(rel))

    recv(xc[3, 1], cx.at[3, hi])
    for s in (1, 2, 4):
        recv(tm[s, 3], tx.at[s, 3])
    lax.fori_loop(0, 10, product(3, False), 0)
    recv(xc[1, 0], cx.at[1, lo])
    for s in (1, 2, 4):
        recv(tm[s, 1], tx.at[s, 1])
    lax.fori_loop(0, 10, product(1, False), 0)
    for s in (1, 2, 4):
        recv(tm[s, 2], tx.at[s, 2])
    recv(xf0, cx.at[2, lo])
    recv(xf1, cx.at[2, hi])
    away = pl.ds(pl.multiple_of((1 - yh) * qw, qw), qw)
    home = pl.ds(pl.multiple_of(yh * qw, qw), qw)
    py = []
    last = product(2, False)
    for s in range(5):
        last(2 * s, 0)
        last(2 * s + 1, 0)
        ps[s] = acc[s, away, :].astype(BF16)
        py.append(send(ps.at[s], pr.at[s], yy))
    for rel in (1, 3, 2):
        recv(ex[rel], er.at[rel - 1])
        eo[...] = eo[...] + er[rel - 1].astype(F32)
    eu = send(eo.at[away], eyu, yy)
    ev = send(eo.at[pl.ds(2 * qw, rank), away], eyv, yy)

    recv(t1, r1)
    recv(t2, r2)
    for c in range(CHUNKS):
        recv(t34[c], r34.at[pl.ds(c * cr, cr)])
    wl[0].wait()

    def total(n, carry):
        cols = pl.ds(pl.multiple_of(n * tile, tile), tile)
        value = dot_nt(cx[0], w[0, cols, :])
        value = value + dot_nt(lf[:, rank:2 * rank], uu[cols, :])
        value = value + r1[:, cols].astype(F32)
        value = value + r2[:, cols].astype(F32)
        gt[:, cols] = value + r34[:, cols].astype(F32)
        return carry

    lax.fori_loop(0, 4, total, 0)
    outs = [load(gt, gt_hbm)]
    for s in range(5):
        recv(py[s], pr.at[s])
        acc[s, home, :] = (acc[s, home, :] + pr[s].astype(F32)) * scale
        outs.append(load(acc.at[s, home, :], gb_hbm.at[s]))
    recv(eu, eyu)
    recv(ev, eyv)
    gu_ref[...] = (eo[home, :] + eyu[...]) * scale
    gv_ref[...] = (eo[pl.ds(2 * qw, rank), home] + eyv[...]) * scale
    for cp in sent:
        cp.wait_send()
    for cp in outs:
        cp.wait()


def per_device(tokens, cotangent, blocks_w, lowrank_u, lowrank_v):
    rows, blk = tokens.shape
    rank = lowrank_u.shape[1]
    slots = blocks_w.shape[1]
    qw = blk // 8
    scale = 1.0 / math.sqrt(rows * lax.axis_size("dp"))
    big = (rows, blk)
    hr = rows // 2
    n_send = 60
    scratch = [
        pltpu.VMEM((4, rows, 2 * qw), BF16),
        pltpu.VMEM((4,) + big, BF16),
        pltpu.VMEM((slots, 4, rows, 2 * qw), BF16),
        pltpu.VMEM((slots, blk, blk), BF16),
        pltpu.VMEM((blk, rank), BF16),
        pltpu.VMEM((rank, blk), BF16),
    ]
    scratch += [pltpu.VMEM(big, BF16)] * 8
    scratch += [
        pltpu.VMEM((slots, 2 * qw, blk), F32),
        pltpu.VMEM((slots, qw, blk), BF16),
        pltpu.VMEM((slots, qw, blk), BF16),
        pltpu.VMEM(big, F32),
        pltpu.VMEM((rows, 2 * rank), F32),
        pltpu.VMEM((hr, 2 * rank), F32),
        pltpu.VMEM((3, hr // 4, 2 * rank), F32),
        pltpu.VMEM((hr // 4, 2 * rank), F32),
        pltpu.VMEM((hr // 4, 2 * rank), F32),
        pltpu.VMEM((rows, 2 * rank), BF16),
        pltpu.VMEM((3, 2 * qw + rank, rank), BF16),
        pltpu.VMEM((3, 2 * qw + rank, rank), BF16),
        pltpu.VMEM((2 * qw + rank, rank), F32),
        pltpu.VMEM((qw, rank), F32),
        pltpu.VMEM((rank, qw), F32),
        pltpu.SemaphoreType.DMA((32,)),
        pltpu.SemaphoreType.DMA((n_send,)),
        pltpu.SemaphoreType.DMA((n_send,)),
    ]
    anyspace = pl.BlockSpec(memory_space=pl.ANY)
    vmem = pl.BlockSpec(memory_space=pltpu.VMEM)
    gt, gb, gu, gv = pl.pallas_call(
        functools.partial(kernel, rows, blk, rank, scale),
        out_shape=(
            jax.ShapeDtypeStruct(big, F32),
            jax.ShapeDtypeStruct((slots, qw, blk), F32),
            jax.ShapeDtypeStruct((qw, rank), F32),
            jax.ShapeDtypeStruct((rank, qw), F32),
        ),
        in_specs=[anyspace] * 5,
        out_specs=(anyspace, anyspace, vmem, vmem),
        scratch_shapes=scratch,
        compiler_params=pltpu.CompilerParams(
            collective_id=0, has_side_effects=True, vmem_limit_bytes=64 << 20
        ),
        name="butterfly",
    )(tokens, cotangent, blocks_w[0], lowrank_u, lowrank_v)
    return gt, jnp.transpose(gb, (1, 0, 2))[:, None], gu, gv


def solution(mesh):
    in_specs = (
        P("dp", "mp"),
        P("dp", "mp"),
        P("mp", None, None, None),
        P("mp", None),
        P(None, "mp"),
    )
    out_specs = (
        P("dp", "mp"),
        P("dp", "mp", None, None),
        P(("mp", "dp"), None),
        P(None, ("mp", "dp")),
    )
    return jax.shard_map(
        per_device, mesh=mesh, in_specs=in_specs, out_specs=out_specs, check_vma=False
    )
```

```python
import functools
import math

import jax
import jax.numpy as jnp
from jax import lax
from jax.experimental import pallas as pl
from jax.experimental.pallas import tpu as pltpu
from jax.sharding import PartitionSpec as P

MESH = pl.DeviceIdType.MESH
F32 = jnp.float32
BF16 = jnp.bfloat16
CHUNKS = 4


def flip(value, bit):
    return value + bit - 2 * bit * lax.rem(lax.div(value, bit), 2)


def dot_nt(a, b):
    return lax.dot_general(a, b, (((1,), (1,)), ((), ())), preferred_element_type=F32)


def dot_tn(a, b):
    return lax.dot_general(a, b, (((0,), (0,)), ((), ())), preferred_element_type=F32)


def kernel(
    rows, blk, rank, scale,
    tok_hbm, cot_hbm, w_hbm, u_hbm, v_hbm,
    gt_hbm, gb_hbm, gu_ref, gv_ref,
    tq, cx, tx, w, uu, vv,
    s4, s34, s2, s1, r4, r34, r2, r1,
    acc, ps, pr, gt, gb,
    lp, lr1, lr2, lz, lr3, lf,
    eb, er, eo, su, sv, eyu, eyv,
    lsem, ssem, rsem,
):
    qw = blk // 8
    dp = lax.axis_index("dp")
    mp = lax.axis_index("mp")
    x = lax.rem(dp, 4)
    yh = lax.div(dp, 4)
    core = lax.rem(mp, 2)
    z = lax.div(mp, 4)

    def px(rel):
        return (yh * 4 + lax.rem(x + rel, 4), mp)

    m1 = (dp, flip(mp, 1))
    m2 = (dp, flip(mp, 2))
    m4 = (dp, flip(mp, 4))
    m8 = (dp, flip(mp, 8))
    m12 = (dp, flip(flip(mp, 4), 8))
    yy = (flip(dp, 4), mp)

    nl = [0]

    def load(src, dst):
        cp = pltpu.make_async_copy(src, dst, lsem.at[nl[0]])
        nl[0] += 1
        cp.start()
        return cp

    barrier = pltpu.get_barrier_semaphore()
    peers = [px(1), px(3), px(2), m1, m2, m4, m8, m12, yy]
    for peer in peers:
        pl.semaphore_signal(barrier, 1, device_id=peer, device_id_type=MESH)
    own = []
    tl = []
    for h in range(2):
        own.append(load(
            tok_hbm.at[:, pl.ds(pl.multiple_of(h * 4 * qw + x * qw, qw), qw)],
            tx.at[0, 0, :, pl.ds(h * qw, qw)],
        ))
    for q in range(4):
        for h in range(2):
            tl.append(load(
                tok_hbm.at[:, pl.ds(h * 4 * qw + q * qw, qw)],
                tq.at[q, :, pl.ds(h * qw, qw)],
            ))
    cl = load(cot_hbm, cx.at[0])
    ul = load(u_hbm, uu)
    vl = load(v_hbm, vv)
    pl.semaphore_wait(barrier, len(peers))

    ns = [0]
    sent = []

    def send(src, dst, peer):
        k = ns[0]
        ns[0] += 1
        cp = pltpu.make_async_remote_copy(
            src_ref=src, dst_ref=dst, send_sem=ssem.at[k], recv_sem=rsem.at[k],
            device_id=peer, device_id_type=MESH,
        )
        cp.start()
        sent.append(cp)
        return k, peer

    def recv(key, dst):
        k, peer = key
        pltpu.make_async_remote_copy(
            src_ref=dst, dst_ref=dst, send_sem=ssem.at[k], recv_sem=rsem.at[k],
            device_id=peer, device_id_type=MESH,
        ).wait_recv()

    tm = {}

    def spread(slot):
        tm[3, slot] = send(tx.at[0, slot], tx.at[3, slot], m4)
        tm[2, slot] = send(tx.at[0, slot], tx.at[2, slot], m2)
        tm[1, slot] = send(tx.at[0, slot], tx.at[1, slot], m1)

    def onward(slot):
        recv(tm[3, slot], tx.at[3, slot])
        tm[4, slot] = send(tx.at[3, slot], tx.at[4, slot], m12)

    for cp in own:
        cp.wait()
    spread(0)
    for cp in tl:
        cp.wait()
    xt = {}
    for rel in (1, 3, 2):
        slot = (4 - rel) % 4
        xt[slot] = send(tq.at[lax.rem(x + rel, 4)], tx.at[0, slot], px(rel))
    cl.wait()
    half = rows // 2
    lo, hi = pl.ds(0, half), pl.ds(half, half)
    xc = {}
    xc[3, 0] = send(cx.at[0, lo], cx.at[3, lo], px(1))
    xc[1, 1] = send(cx.at[0, hi], cx.at[1, hi], px(3))
    xc[3, 1] = send(cx.at[0, hi], cx.at[3, hi], px(1))
    xc[1, 0] = send(cx.at[0, lo], cx.at[1, lo], px(3))
    wl = {s: load(w_hbm.at[s], w.at[s]) for s in (4, 2, 3, 1, 0)}

    ul.wait()
    vl.wait()
    low = jnp.zeros((rows, rank), F32)
    for q in range(4):
        uq = jnp.concatenate(
            [uu[q * qw:(q + 1) * qw, :], uu[(4 + q) * qw:(5 + q) * qw, :]], axis=0
        )
        low = low + jnp.dot(tq[q], uq, preferred_element_type=F32)
    lp[:, 0:rank] = low
    lp[:, rank:2 * rank] = dot_nt(cx[0], vv[...])
    hr = rows // 2
    zr = hr // 4
    mine = pl.ds(pl.multiple_of(core * hr, hr), hr)
    other = pl.ds(pl.multiple_of((1 - core) * hr, hr), hr)
    a1 = send(lp.at[other], lr1, m1)

    tile = blk // 4

    def term(slot, out, first, count, extra=None):
        at = pl.ds(first, count)

        def step(n, carry):
            cols = pl.ds(pl.multiple_of(n * tile, tile), tile)
            value = dot_nt(cx[0, at, :], w[slot, cols, :])
            if extra is not None:
                value = value + extra[at, cols].astype(F32)
            out[at, cols] = value.astype(BF16)
            return carry

        lax.fori_loop(0, 4, step, 0)

    def along(v):
        zz = z
        if v & 1:
            zz = flip(zz, 1)
        if v & 2:
            zz = flip(zz, 2)
        return zz

    hops = ((1, m4), (3, m12), (2, m8))
    cr = rows // CHUNKS
    wl[4].wait()
    t4 = []

    def fourth(c):
        term(4, s4, c * cr, cr)
        at = pl.ds(c * cr, cr)
        t4.append(send(s4.at[at], r4.at[at], m12))

    fourth(0)
    recv(a1, lr1)
    lr1[...] = lr1[...] + lp[mine, :]
    a2 = {}
    for v, peer in hops:
        a2[v] = send(
            lr1.at[pl.ds(pl.multiple_of(along(v) * zr, zr), zr)], lr2.at[v - 1], peer
        )
    fourth(1)
    t34 = []

    def chain(c):
        at = pl.ds(c * cr, cr)
        recv(t4[c], r4.at[at])
        term(3, s34, c * cr, cr, r4)
        t34.append(send(s34.at[at], r34.at[at], m4))

    wide = blk // 2

    def product(slot, first):
        def step(i, carry):
            s = lax.div(i, 2)
            cols = pl.ds(pl.multiple_of(lax.rem(i, 2) * wide, wide), wide)
            value = dot_tn(tx[s, slot], cx[slot, :, cols])
            if first:
                acc[s, :, cols] = value
            else:
                acc[s, :, cols] = acc[s, :, cols] + value
            return carry
        return step


    def multiply(slot, first):
        for s in (1, 2, 4):
            recv(tm[s, slot], tx.at[s, slot])
        lax.fori_loop(0, 10, product(slot, first), 0)

    for slot in (3, 1):
        recv(xt[slot], tx.at[0, slot])
        spread(slot)
    onward(0)
    for v, peer in hops:
        recv(a2[v], lr2.at[v - 1])
    lz[...] = (
        lr1[pl.ds(pl.multiple_of(z * zr, zr), zr), :] + lr2[0] + lr2[1] + lr2[2]
    )
    a3 = send(lz, lr3, m2)
    recv(xt[2], tx.at[0, 2])
    spread(2)
    wl[2].wait()
    term(2, s2, 0, rows)
    t2 = send(s2, r2, m2)
    wl[1].wait()
    term(1, s1, 0, rows)
    t1 = send(s1, r1, m1)
    onward(3)
    onward(1)
    recv(a3, lr3)
    piece = pl.ds(pl.multiple_of(core * hr + z * zr, zr), zr)
    lf[piece, :] = (lz[...] + lr3[...]).astype(BF16)
    a4 = {}
    for v, peer in hops:
        a4[v] = send(lf.at[piece], lf.at[piece], peer)
    fourth(2)
    wl[3].wait()
    recv(xc[3, 0], cx.at[3, lo])
    xf0 = send(cx.at[3, lo], cx.at[2, lo], px(1))
    recv(xc[1, 1], cx.at[1, hi])
    xf1 = send(cx.at[1, hi], cx.at[2, hi], px(3))
    chain(0)
    chain(1)
    onward(2)
    fourth(3)
    multiply(0, True)
    recv(xc[3, 1], cx.at[3, hi])
    multiply(3, False)
    recv(xc[1, 0], cx.at[1, lo])
    multiply(1, False)
    for v, peer in hops:
        recv(a4[v], lf.at[pl.ds(pl.multiple_of(core * hr + along(v) * zr, zr), zr)])
    a5 = send(lf.at[mine], lf.at[mine], m1)
    chain(2)
    recv(a5, lf.at[other])
    ex = {}
    for rel in (1, 3, 2, 0):
        q = lax.rem(x + rel, 4)
        gu = dot_tn(tq[q], lf[:, rank:2 * rank])
        ga = dot_tn(lf[:, 0:rank], cx[0, :, pl.ds(pl.multiple_of(q * qw, qw), qw)])
        gc = dot_tn(lf[:, 0:rank], cx[0, :, pl.ds(pl.multiple_of(4 * qw + q * qw, qw), qw)])
        if rel == 0:
            eo[0:2 * qw, :] = gu
            eo[2 * qw:2 * qw + rank, 0:qw] = ga
            eo[2 * qw:2 * qw + rank, qw:2 * qw] = gc
        else:
            eb[rel - 1, 0:2 * qw, :] = gu.astype(BF16)
            eb[rel - 1, 2 * qw:2 * qw + rank, 0:qw] = ga.astype(BF16)
            eb[rel - 1, 2 * qw:2 * qw + rank, qw:2 * qw] = gc.astype(BF16)
            ex[rel] = send(eb.at[rel - 1], er.at[rel - 1], px(rel))

    for s in (1, 2):
        recv(tm[s, 2], tx.at[s, 2])
    recv(xf0, cx.at[2, lo])
    recv(xf1, cx.at[2, hi])
    away = pl.ds(pl.multiple_of((1 - yh) * qw, qw), qw)
    home = pl.ds(pl.multiple_of(yh * qw, qw), qw)
    py = []
    last = product(2, False)

    def close(s):
        last(2 * s, 0)
        last(2 * s + 1, 0)
        ps[s] = acc[s, away, :].astype(BF16)
        py.append(send(ps.at[s], pr.at[s], yy))

    close(0)
    close(1)
    close(2)
    close(3)
    for rel in (1, 3, 2):
        recv(ex[rel], er.at[rel - 1])
        eo[...] = eo[...] + er[rel - 1].astype(F32)
    su[...] = eo[away, :].astype(BF16)
    sv[...] = eo[pl.ds(2 * qw, rank), away].astype(BF16)
    eu = send(su, eyu, yy)
    ev = send(sv, eyv, yy)
    recv(tm[4, 2], tx.at[4, 2])
    close(4)
    chain(3)

    recv(t1, r1)
    recv(t2, r2)
    for c in range(CHUNKS):
        recv(t34[c], r34.at[pl.ds(c * cr, cr)])
    wl[0].wait()

    def total(n, carry):
        cols = pl.ds(pl.multiple_of(n * tile, tile), tile)
        value = dot_nt(cx[0], w[0, cols, :])
        value = value + dot_nt(lf[:, rank:2 * rank], uu[cols, :])
        value = value + r1[:, cols].astype(F32)
        value = value + r2[:, cols].astype(F32)
        gt[:, cols] = value + r34[:, cols].astype(F32)
        return carry

    lax.fori_loop(0, 4, total, 0)
    outs = [load(gt, gt_hbm)]
    for s in range(5):
        recv(py[s], pr.at[s])
        value = (acc[s, home, :] + pr[s].astype(F32)) * scale
        gb[s] = value.reshape(qw, 1, blk)
        outs.append(load(gb.at[s], gb_hbm.at[:, s]))
    recv(eu, eyu)
    recv(ev, eyv)
    gu_ref[...] = (eo[home, :] + eyu[...].astype(F32)) * scale
    gv_ref[...] = (eo[pl.ds(2 * qw, rank), home] + eyv[...].astype(F32)) * scale
    for cp in sent:
        cp.wait_send()
    for cp in outs:
        cp.wait()


def per_device(tokens, cotangent, blocks_w, lowrank_u, lowrank_v):
    rows, blk = tokens.shape
    rank = lowrank_u.shape[1]
    slots = blocks_w.shape[1]
    qw = blk // 8
    scale = 1.0 / math.sqrt(rows * lax.axis_size("dp"))
    big = (rows, blk)
    hr = rows // 2
    n_send = 60
    scratch = [
        pltpu.VMEM((4, rows, 2 * qw), BF16),
        pltpu.VMEM((4,) + big, BF16),
        pltpu.VMEM((slots, 4, rows, 2 * qw), BF16),
        pltpu.VMEM((slots, blk, blk), BF16),
        pltpu.VMEM((blk, rank), BF16),
        pltpu.VMEM((rank, blk), BF16),
    ]
    scratch += [pltpu.VMEM(big, BF16)] * 8
    scratch += [
        pltpu.VMEM((slots, 2 * qw, blk), F32),
        pltpu.VMEM((slots, qw, blk), BF16),
        pltpu.VMEM((slots, qw, blk), BF16),
        pltpu.VMEM(big, F32),
        pltpu.VMEM((slots, qw, 1, blk), F32),
        pltpu.VMEM((rows, 2 * rank), F32),
        pltpu.VMEM((hr, 2 * rank), F32),
        pltpu.VMEM((3, hr // 4, 2 * rank), F32),
        pltpu.VMEM((hr // 4, 2 * rank), F32),
        pltpu.VMEM((hr // 4, 2 * rank), F32),
        pltpu.VMEM((rows, 2 * rank), BF16),
        pltpu.VMEM((3, 2 * qw + rank, rank), BF16),
        pltpu.VMEM((3, 2 * qw + rank, rank), BF16),
        pltpu.VMEM((2 * qw + rank, rank), F32),
        pltpu.VMEM((qw, rank), BF16),
        pltpu.VMEM((rank, qw), BF16),
        pltpu.VMEM((qw, rank), BF16),
        pltpu.VMEM((rank, qw), BF16),
        pltpu.SemaphoreType.DMA((32,)),
        pltpu.SemaphoreType.DMA((n_send,)),
        pltpu.SemaphoreType.DMA((n_send,)),
    ]
    anyspace = pl.BlockSpec(memory_space=pl.ANY)
    vmem = pl.BlockSpec(memory_space=pltpu.VMEM)
    gt, gb, gu, gv = pl.pallas_call(
        functools.partial(kernel, rows, blk, rank, scale),
        out_shape=(
            jax.ShapeDtypeStruct(big, F32),
            jax.ShapeDtypeStruct((qw, slots, 1, blk), F32),
            jax.ShapeDtypeStruct((qw, rank), F32),
            jax.ShapeDtypeStruct((rank, qw), F32),
        ),
        in_specs=[anyspace] * 5,
        out_specs=(anyspace, anyspace, vmem, vmem),
        scratch_shapes=scratch,
        compiler_params=pltpu.CompilerParams(
            collective_id=0, has_side_effects=True, vmem_limit_bytes=64 << 20
        ),
        name="butterfly",
    )(tokens, cotangent, blocks_w[0], lowrank_u, lowrank_v)
    return gt, jnp.transpose(gb, (0, 2, 1, 3)), gu, gv


def solution(mesh):
    in_specs = (
        P("dp", "mp"),
        P("dp", "mp"),
        P("mp", None, None, None),
        P("mp", None),
        P(None, "mp"),
    )
    out_specs = (
        P("dp", "mp"),
        P("dp", "mp", None, None),
        P(("mp", "dp"), None),
        P(None, ("mp", "dp")),
    )
    return jax.shard_map(
        per_device, mesh=mesh, in_specs=in_specs, out_specs=out_specs, check_vma=False
    )
```

```python
import functools
import math

import jax
import jax.numpy as jnp
from jax import lax
from jax.experimental import pallas as pl
from jax.experimental.pallas import tpu as pltpu
from jax.sharding import PartitionSpec as P

MESH = pl.DeviceIdType.MESH
F32 = jnp.float32
BF16 = jnp.bfloat16
CHUNKS = 4


def flip(value, bit):
    return value + bit - 2 * bit * lax.rem(lax.div(value, bit), 2)


def dot_nt(a, b):
    return lax.dot_general(a, b, (((1,), (1,)), ((), ())), preferred_element_type=F32)


def dot_tn(a, b):
    return lax.dot_general(a, b, (((0,), (0,)), ((), ())), preferred_element_type=F32)


def kernel(
    rows, blk, rank, scale,
    tok_hbm, cot_hbm, w_hbm, u_hbm, v_hbm,
    gt_hbm, gb_hbm, gu_ref, gv_ref,
    tq, cx, tx, w, uu, vv,
    s4, s34, s2, s1, r4, r34, r2, r1,
    acc, ps, pr, gt, gb,
    lp, lr1, lr2, lz, lr3, lf,
    eb, er, eo, su, sv, eyu, eyv,
    lsem, ssem, rsem,
):
    qw = blk // 8
    dp = lax.axis_index("dp")
    mp = lax.axis_index("mp")
    x = lax.rem(dp, 4)
    yh = lax.div(dp, 4)
    core = lax.rem(mp, 2)
    z = lax.div(mp, 4)

    def px(rel):
        return (yh * 4 + lax.rem(x + rel, 4), mp)

    m1 = (dp, flip(mp, 1))
    m2 = (dp, flip(mp, 2))
    m4 = (dp, flip(mp, 4))
    m8 = (dp, flip(mp, 8))
    m12 = (dp, flip(flip(mp, 4), 8))
    yy = (flip(dp, 4), mp)

    nl = [0]

    def load(src, dst):
        cp = pltpu.make_async_copy(src, dst, lsem.at[nl[0]])
        nl[0] += 1
        cp.start()
        return cp

    barrier = pltpu.get_barrier_semaphore()
    peers = [px(1), px(3), px(2), m1, m2, m4, m8, m12, yy]
    for peer in peers:
        pl.semaphore_signal(barrier, 1, device_id=peer, device_id_type=MESH)
    own = []
    tl = []
    for h in range(2):
        own.append(load(
            tok_hbm.at[:, pl.ds(pl.multiple_of(h * 4 * qw + x * qw, qw), qw)],
            tx.at[0, 0, :, pl.ds(h * qw, qw)],
        ))
    for q in range(4):
        for h in range(2):
            tl.append(load(
                tok_hbm.at[:, pl.ds(h * 4 * qw + q * qw, qw)],
                tq.at[q, :, pl.ds(h * qw, qw)],
            ))
    cl = load(cot_hbm, cx.at[0])
    ul = load(u_hbm, uu)
    vl = load(v_hbm, vv)
    pl.semaphore_wait(barrier, len(peers))

    ns = [0]
    sent = []

    def send(src, dst, peer):
        k = ns[0]
        ns[0] += 1
        cp = pltpu.make_async_remote_copy(
            src_ref=src, dst_ref=dst, send_sem=ssem.at[k], recv_sem=rsem.at[k],
            device_id=peer, device_id_type=MESH,
        )
        cp.start()
        sent.append(cp)
        return k, peer

    def recv(key, dst):
        k, peer = key
        pltpu.make_async_remote_copy(
            src_ref=dst, dst_ref=dst, send_sem=ssem.at[k], recv_sem=rsem.at[k],
            device_id=peer, device_id_type=MESH,
        ).wait_recv()

    tm = {}

    def spread(slot):
        tm[3, slot] = send(tx.at[0, slot], tx.at[3, slot], m4)
        tm[2, slot] = send(tx.at[0, slot], tx.at[2, slot], m2)
        tm[1, slot] = send(tx.at[0, slot], tx.at[1, slot], m1)

    def onward(slot):
        recv(tm[3, slot], tx.at[3, slot])
        tm[4, slot] = send(tx.at[3, slot], tx.at[4, slot], m12)

    for cp in own:
        cp.wait()
    spread(0)
    for cp in tl:
        cp.wait()
    xt = {}
    for rel in (1, 3, 2):
        slot = (4 - rel) % 4
        xt[slot] = send(tq.at[lax.rem(x + rel, 4)], tx.at[0, slot], px(rel))
    cl.wait()
    half = rows // 2
    wide = blk // 2
    lo, hi = pl.ds(0, half), pl.ds(half, half)
    side = (pl.ds(0, wide), pl.ds(wide, wide))
    xc = {}
    for g in range(2):
        xc[3, g] = send(cx.at[0, :, side[g]], cx.at[3, :, side[g]], px(1))
        xc[1, g] = send(cx.at[0, :, side[g]], cx.at[1, :, side[g]], px(3))
    wl = {s: load(w_hbm.at[s], w.at[s]) for s in (4, 2, 3, 1, 0)}

    ul.wait()
    vl.wait()
    low = jnp.zeros((rows, rank), F32)
    for q in range(4):
        uq = jnp.concatenate(
            [uu[q * qw:(q + 1) * qw, :], uu[(4 + q) * qw:(5 + q) * qw, :]], axis=0
        )
        low = low + jnp.dot(tq[q], uq, preferred_element_type=F32)
    lp[:, 0:rank] = low
    lp[:, rank:2 * rank] = dot_nt(cx[0], vv[...])
    hr = rows // 2
    zr = hr // 4
    mine = pl.ds(pl.multiple_of(core * hr, hr), hr)
    other = pl.ds(pl.multiple_of((1 - core) * hr, hr), hr)
    a1 = send(lp.at[other], lr1, m1)

    tile = blk // 4

    def term(slot, out, first, count, extra=None):
        at = pl.ds(first, count)

        def step(n, carry):
            cols = pl.ds(pl.multiple_of(n * tile, tile), tile)
            value = dot_nt(cx[0, at, :], w[slot, cols, :])
            if extra is not None:
                value = value + extra[at, cols].astype(F32)
            out[at, cols] = value.astype(BF16)
            return carry

        lax.fori_loop(0, 4, step, 0)

    def along(v):
        zz = z
        if v & 1:
            zz = flip(zz, 1)
        if v & 2:
            zz = flip(zz, 2)
        return zz

    hops = ((1, m4), (3, m12), (2, m8))
    cr = rows // CHUNKS
    wl[4].wait()
    t4 = []

    def fourth(c):
        term(4, s4, c * cr, cr)
        at = pl.ds(c * cr, cr)
        t4.append(send(s4.at[at], r4.at[at], m12))

    fourth(0)
    recv(a1, lr1)
    lr1[...] = lr1[...] + lp[mine, :]
    a2 = {}
    for v, peer in hops:
        a2[v] = send(
            lr1.at[pl.ds(pl.multiple_of(along(v) * zr, zr), zr)], lr2.at[v - 1], peer
        )
    fourth(1)
    t34 = []

    def chain(c):
        at = pl.ds(c * cr, cr)
        recv(t4[c], r4.at[at])
        term(3, s34, c * cr, cr, r4)
        t34.append(send(s34.at[at], r34.at[at], m4))

    def product(slot, g, first):
        def step(s, carry):
            value = dot_tn(tx[s, slot], cx[slot, :, side[g]])
            if first:
                acc[s, :, side[g]] = value
            else:
                acc[s, :, side[g]] = acc[s, :, side[g]] + value
            return carry
        return step

    xf = {}

    def pass_on(g):
        recv(xc[3, g], cx.at[3, :, side[g]])
        xf[0, g] = send(cx.at[3, lo, side[g]], cx.at[2, lo, side[g]], px(1))
        recv(xc[1, g], cx.at[1, :, side[g]])
        xf[1, g] = send(cx.at[1, hi, side[g]], cx.at[2, hi, side[g]], px(3))

    def multiply(slot, first):
        for s in (1, 2, 4):
            recv(tm[s, slot], tx.at[s, slot])
        for g in range(2):
            lax.fori_loop(0, 5, product(slot, g, first), 0)

    for slot in (3, 1):
        recv(xt[slot], tx.at[0, slot])
        spread(slot)
    onward(0)
    for v, peer in hops:
        recv(a2[v], lr2.at[v - 1])
    lz[...] = (
        lr1[pl.ds(pl.multiple_of(z * zr, zr), zr), :] + lr2[0] + lr2[1] + lr2[2]
    )
    a3 = send(lz, lr3, m2)
    recv(xt[2], tx.at[0, 2])
    spread(2)
    wl[2].wait()
    term(2, s2, 0, rows)
    t2 = send(s2, r2, m2)
    wl[1].wait()
    term(1, s1, 0, rows)
    t1 = send(s1, r1, m1)
    onward(3)
    onward(1)
    recv(a3, lr3)
    piece = pl.ds(pl.multiple_of(core * hr + z * zr, zr), zr)
    lf[piece, :] = (lz[...] + lr3[...]).astype(BF16)
    a4 = {}
    for v, peer in hops:
        a4[v] = send(lf.at[piece], lf.at[piece], peer)
    fourth(2)
    wl[3].wait()
    pass_on(0)
    chain(0)
    chain(1)
    onward(2)
    fourth(3)
    multiply(0, True)
    pass_on(1)
    multiply(3, False)
    multiply(1, False)
    away = pl.ds(pl.multiple_of((1 - yh) * qw, qw), qw)
    home = pl.ds(pl.multiple_of(yh * qw, qw), qw)
    py = {}

    def close(s, g):
        product(2, g, False)(s, 0)
        ps[s, :, side[g]] = acc[s, away, side[g]].astype(BF16)
        py[s, g] = send(ps.at[s, :, side[g]], pr.at[s, :, side[g]], yy)

    for s in (1, 2):
        recv(tm[s, 2], tx.at[s, 2])
    for v, peer in hops:
        recv(a4[v], lf.at[pl.ds(pl.multiple_of(core * hr + along(v) * zr, zr), zr)])
    a5 = send(lf.at[mine], lf.at[mine], m1)
    for g in range(2):
        recv(xf[0, g], cx.at[2, lo, side[g]])
        recv(xf[1, g], cx.at[2, hi, side[g]])
        for s in range(4):
            close(s, g)
    recv(tm[4, 2], tx.at[4, 2])
    close(4, 0)
    close(4, 1)
    recv(a5, lf.at[other])
    ex = {}
    for rel in (1, 3, 2, 0):
        q = lax.rem(x + rel, 4)
        gu = dot_tn(tq[q], lf[:, rank:2 * rank])
        ga = dot_tn(lf[:, 0:rank], cx[0, :, pl.ds(pl.multiple_of(q * qw, qw), qw)])
        gc = dot_tn(lf[:, 0:rank], cx[0, :, pl.ds(pl.multiple_of(4 * qw + q * qw, qw), qw)])
        if rel == 0:
            eo[0:2 * qw, :] = gu
            eo[2 * qw:2 * qw + rank, 0:qw] = ga
            eo[2 * qw:2 * qw + rank, qw:2 * qw] = gc
        else:
            eb[rel - 1, 0:2 * qw, :] = gu.astype(BF16)
            eb[rel - 1, 2 * qw:2 * qw + rank, 0:qw] = ga.astype(BF16)
            eb[rel - 1, 2 * qw:2 * qw + rank, qw:2 * qw] = gc.astype(BF16)
            ex[rel] = send(eb.at[rel - 1], er.at[rel - 1], px(rel))

    chain(2)
    chain(3)
    for rel in (1, 3, 2):
        recv(ex[rel], er.at[rel - 1])
        eo[...] = eo[...] + er[rel - 1].astype(F32)
    su[...] = eo[away, :].astype(BF16)
    sv[...] = eo[pl.ds(2 * qw, rank), away].astype(BF16)
    eu = send(su, eyu, yy)
    ev = send(sv, eyv, yy)

    recv(t1, r1)
    recv(t2, r2)
    for c in range(CHUNKS):
        recv(t34[c], r34.at[pl.ds(c * cr, cr)])
    wl[0].wait()

    def total(n, carry):
        cols = pl.ds(pl.multiple_of(n * tile, tile), tile)
        value = dot_nt(cx[0], w[0, cols, :])
        value = value + dot_nt(lf[:, rank:2 * rank], uu[cols, :])
        value = value + r1[:, cols].astype(F32)
        value = value + r2[:, cols].astype(F32)
        gt[:, cols] = value + r34[:, cols].astype(F32)
        return carry

    lax.fori_loop(0, 4, total, 0)
    outs = [load(gt, gt_hbm)]
    for s in range(5):
        for g in range(2):
            recv(py[s, g], pr.at[s, :, side[g]])
        value = (acc[s, home, :] + pr[s].astype(F32)) * scale
        gb[s] = value.reshape(qw, 1, blk)
        outs.append(load(gb.at[s], gb_hbm.at[:, s]))
    recv(eu, eyu)
    recv(ev, eyv)
    gu_ref[...] = (eo[home, :] + eyu[...].astype(F32)) * scale
    gv_ref[...] = (eo[pl.ds(2 * qw, rank), home] + eyv[...].astype(F32)) * scale
    for cp in sent:
        cp.wait_send()
    for cp in outs:
        cp.wait()


def per_device(tokens, cotangent, blocks_w, lowrank_u, lowrank_v):
    rows, blk = tokens.shape
    rank = lowrank_u.shape[1]
    slots = blocks_w.shape[1]
    qw = blk // 8
    scale = 1.0 / math.sqrt(rows * lax.axis_size("dp"))
    big = (rows, blk)
    hr = rows // 2
    n_send = 64
    scratch = [
        pltpu.VMEM((4, rows, 2 * qw), BF16),
        pltpu.VMEM((4,) + big, BF16),
        pltpu.VMEM((slots, 4, rows, 2 * qw), BF16),
        pltpu.VMEM((slots, blk, blk), BF16),
        pltpu.VMEM((blk, rank), BF16),
        pltpu.VMEM((rank, blk), BF16),
    ]
    scratch += [pltpu.VMEM(big, BF16)] * 8
    scratch += [
        pltpu.VMEM((slots, 2 * qw, blk), F32),
        pltpu.VMEM((slots, qw, blk), BF16),
        pltpu.VMEM((slots, qw, blk), BF16),
        pltpu.VMEM(big, F32),
        pltpu.VMEM((slots, qw, 1, blk), F32),
        pltpu.VMEM((rows, 2 * rank), F32),
        pltpu.VMEM((hr, 2 * rank), F32),
        pltpu.VMEM((3, hr // 4, 2 * rank), F32),
        pltpu.VMEM((hr // 4, 2 * rank), F32),
        pltpu.VMEM((hr // 4, 2 * rank), F32),
        pltpu.VMEM((rows, 2 * rank), BF16),
        pltpu.VMEM((3, 2 * qw + rank, rank), BF16),
        pltpu.VMEM((3, 2 * qw + rank, rank), BF16),
        pltpu.VMEM((2 * qw + rank, rank), F32),
        pltpu.VMEM((qw, rank), BF16),
        pltpu.VMEM((rank, qw), BF16),
        pltpu.VMEM((qw, rank), BF16),
        pltpu.VMEM((rank, qw), BF16),
        pltpu.SemaphoreType.DMA((32,)),
        pltpu.SemaphoreType.DMA((n_send,)),
        pltpu.SemaphoreType.DMA((n_send,)),
    ]
    anyspace = pl.BlockSpec(memory_space=pl.ANY)
    vmem = pl.BlockSpec(memory_space=pltpu.VMEM)
    gt, gb, gu, gv = pl.pallas_call(
        functools.partial(kernel, rows, blk, rank, scale),
        out_shape=(
            jax.ShapeDtypeStruct(big, F32),
            jax.ShapeDtypeStruct((qw, slots, 1, blk), F32),
            jax.ShapeDtypeStruct((qw, rank), F32),
            jax.ShapeDtypeStruct((rank, qw), F32),
        ),
        in_specs=[anyspace] * 5,
        out_specs=(anyspace, anyspace, vmem, vmem),
        scratch_shapes=scratch,
        compiler_params=pltpu.CompilerParams(
            collective_id=0, has_side_effects=True, vmem_limit_bytes=64 << 20
        ),
        name="butterfly",
    )(tokens, cotangent, blocks_w[0], lowrank_u, lowrank_v)
    return gt, jnp.transpose(gb, (0, 2, 1, 3)), gu, gv


def solution(mesh):
    in_specs = (
        P("dp", "mp"),
        P("dp", "mp"),
        P("mp", None, None, None),
        P("mp", None),
        P(None, "mp"),
    )
    out_specs = (
        P("dp", "mp"),
        P("dp", "mp", None, None),
        P(("mp", "dp"), None),
        P(None, ("mp", "dp")),
    )
    return jax.shard_map(
        per_device, mesh=mesh, in_specs=in_specs, out_specs=out_specs, check_vma=False
    )
```

```python
import functools
import math

import jax
import jax.numpy as jnp
from jax import lax
from jax.experimental import pallas as pl
from jax.experimental.pallas import tpu as pltpu
from jax.sharding import PartitionSpec as P

MESH = pl.DeviceIdType.MESH
F32 = jnp.float32
BF16 = jnp.bfloat16
CHUNKS = 4


def flip(value, bit):
    return value + bit - 2 * bit * lax.rem(lax.div(value, bit), 2)


def dot_nt(a, b):
    return lax.dot_general(a, b, (((1,), (1,)), ((), ())), preferred_element_type=F32)


def dot_tn(a, b):
    return lax.dot_general(a, b, (((0,), (0,)), ((), ())), preferred_element_type=F32)


def kernel(
    rows, blk, rank, scale,
    tok_hbm, cot_hbm, w_hbm, u_hbm, v_hbm,
    gt_hbm, gb_hbm, gu_ref, gv_ref,
    tq, cx, tx, w, uu, vv,
    s4, s34, s2, s1, r4, r34, r2, r1,
    acc, ps, pr, gt, gb,
    lp, lr1, lr2, lz, lr3, lf,
    eb, er, eo, su, sv, eyu, eyv,
    lsem, ssem, rsem,
):
    qw = blk // 8
    dp = lax.axis_index("dp")
    mp = lax.axis_index("mp")
    x = lax.rem(dp, 4)
    yh = lax.div(dp, 4)
    core = lax.rem(mp, 2)
    z = lax.div(mp, 4)

    def px(rel):
        return (yh * 4 + lax.rem(x + rel, 4), mp)

    m1 = (dp, flip(mp, 1))
    m2 = (dp, flip(mp, 2))
    m4 = (dp, flip(mp, 4))
    m8 = (dp, flip(mp, 8))
    m12 = (dp, flip(flip(mp, 4), 8))
    yy = (flip(dp, 4), mp)

    nl = [0]

    def load(src, dst):
        cp = pltpu.make_async_copy(src, dst, lsem.at[nl[0]])
        nl[0] += 1
        cp.start()
        return cp

    barrier = pltpu.get_barrier_semaphore()
    peers = [px(1), px(3), px(2), m1, m2, m4, m8, m12, yy]
    for peer in peers:
        pl.semaphore_signal(barrier, 1, device_id=peer, device_id_type=MESH)
    own = []
    tl = []
    for h in range(2):
        own.append(load(
            tok_hbm.at[:, pl.ds(pl.multiple_of(h * 4 * qw + x * qw, qw), qw)],
            tx.at[0, 0, :, pl.ds(h * qw, qw)],
        ))
    for q in range(4):
        for h in range(2):
            tl.append(load(
                tok_hbm.at[:, pl.ds(h * 4 * qw + q * qw, qw)],
                tq.at[q, :, pl.ds(h * qw, qw)],
            ))
    cl = load(cot_hbm, cx.at[0])
    ul = load(u_hbm, uu)
    vl = load(v_hbm, vv)
    pl.semaphore_wait(barrier, len(peers))

    ns = [0]
    sent = []

    def send(src, dst, peer):
        k = ns[0]
        ns[0] += 1
        cp = pltpu.make_async_remote_copy(
            src_ref=src, dst_ref=dst, send_sem=ssem.at[k], recv_sem=rsem.at[k],
            device_id=peer, device_id_type=MESH,
        )
        cp.start()
        sent.append(cp)
        return k, peer

    def recv(key, dst):
        k, peer = key
        pltpu.make_async_remote_copy(
            src_ref=dst, dst_ref=dst, send_sem=ssem.at[k], recv_sem=rsem.at[k],
            device_id=peer, device_id_type=MESH,
        ).wait_recv()

    tm = {}

    def spread(slot):
        tm[3, slot] = send(tx.at[0, slot], tx.at[3, slot], m4)
        tm[2, slot] = send(tx.at[0, slot], tx.at[2, slot], m2)
        tm[1, slot] = send(tx.at[0, slot], tx.at[1, slot], m1)

    def onward(slot):
        recv(tm[3, slot], tx.at[3, slot])
        tm[4, slot] = send(tx.at[3, slot], tx.at[4, slot], m12)

    for cp in own:
        cp.wait()
    spread(0)
    for cp in tl:
        cp.wait()
    xt = {}
    for rel in (1, 3, 2):
        slot = (4 - rel) % 4
        xt[slot] = send(tq.at[lax.rem(x + rel, 4)], tx.at[0, slot], px(rel))
    cl.wait()
    half = rows // 2
    wide = blk // 2
    lo, hi = pl.ds(0, half), pl.ds(half, half)
    side = (pl.ds(0, wide), pl.ds(wide, wide))
    xc = {}
    for g in range(2):
        xc[3, g] = send(cx.at[0, :, side[g]], cx.at[3, :, side[g]], px(1))
        xc[1, g] = send(cx.at[0, :, side[g]], cx.at[1, :, side[g]], px(3))
    wl = {s: load(w_hbm.at[s], w.at[s]) for s in (4, 2, 3, 1, 0)}

    ul.wait()
    vl.wait()
    low = jnp.zeros((rows, rank), F32)
    for q in range(4):
        uq = jnp.concatenate(
            [uu[q * qw:(q + 1) * qw, :], uu[(4 + q) * qw:(5 + q) * qw, :]], axis=0
        )
        low = low + jnp.dot(tq[q], uq, preferred_element_type=F32)
    lp[:, 0:rank] = low
    lp[:, rank:2 * rank] = dot_nt(cx[0], vv[...])
    hr = rows // 2
    zr = hr // 4
    mine = pl.ds(pl.multiple_of(core * hr, hr), hr)
    other = pl.ds(pl.multiple_of((1 - core) * hr, hr), hr)
    a1 = send(lp.at[other], lr1, m1)

    tile = blk // 4

    def term(slot, out, first, count, extra=None):
        at = pl.ds(first, count)

        def step(n, carry):
            cols = pl.ds(pl.multiple_of(n * tile, tile), tile)
            value = dot_nt(cx[0, at, :], w[slot, cols, :])
            if extra is not None:
                value = value + extra[at, cols].astype(F32)
            out[at, cols] = value.astype(BF16)
            return carry

        lax.fori_loop(0, 4, step, 0)

    def along(v):
        zz = z
        if v & 1:
            zz = flip(zz, 1)
        if v & 2:
            zz = flip(zz, 2)
        return zz

    hops = ((1, m4), (3, m12), (2, m8))
    cr = rows // CHUNKS
    wl[4].wait()
    t4 = []

    def fourth(c):
        term(4, s4, c * cr, cr)
        at = pl.ds(c * cr, cr)
        t4.append(send(s4.at[at], r4.at[at], m12))

    fourth(0)
    recv(a1, lr1)
    lr1[...] = lr1[...] + lp[mine, :]
    a2 = {}
    for v, peer in hops:
        a2[v] = send(
            lr1.at[pl.ds(pl.multiple_of(along(v) * zr, zr), zr)], lr2.at[v - 1], peer
        )
    fourth(1)
    t34 = []

    def chain(c):
        at = pl.ds(c * cr, cr)
        recv(t4[c], r4.at[at])
        term(3, s34, c * cr, cr, r4)
        t34.append(send(s34.at[at], r34.at[at], m4))

    def product(slot, g, first):
        def step(s, carry):
            value = dot_tn(tx[s, slot], cx[slot, :, side[g]])
            if first:
                acc[s, :, side[g]] = value
            else:
                acc[s, :, side[g]] = acc[s, :, side[g]] + value
            return carry
        return step

    xf = {}

    def pass_on(g):
        recv(xc[3, g], cx.at[3, :, side[g]])
        xf[0, g] = send(cx.at[3, lo, side[g]], cx.at[2, lo, side[g]], px(1))
        recv(xc[1, g], cx.at[1, :, side[g]])
        xf[1, g] = send(cx.at[1, hi, side[g]], cx.at[2, hi, side[g]], px(3))

    def multiply(slot, first):
        for s in (1, 2, 4):
            recv(tm[s, slot], tx.at[s, slot])
        for g in range(2):
            lax.fori_loop(0, 5, product(slot, g, first), 0)

    for slot in (3, 1):
        recv(xt[slot], tx.at[0, slot])
        spread(slot)
    onward(0)
    for v, peer in hops:
        recv(a2[v], lr2.at[v - 1])
    lz[...] = (
        lr1[pl.ds(pl.multiple_of(z * zr, zr), zr), :] + lr2[0] + lr2[1] + lr2[2]
    )
    yl = lax.rem(lax.div(mp, 2), 2)
    hz = zr // 2
    a3 = send(lz.at[pl.ds(pl.multiple_of((1 - yl) * hz, hz), hz)], lr3, m2)
    recv(xt[2], tx.at[0, 2])
    spread(2)
    wl[2].wait()
    term(2, s2, 0, rows)
    t2 = [send(s2.at[lo], r2.at[lo], m2)]
    wl[1].wait()
    term(1, s1, 0, rows)
    t1 = send(s1, r1, m1)
    onward(3)
    onward(1)
    recv(a3, lr3)
    piece = pl.ds(pl.multiple_of(core * hr + z * zr, zr), zr)
    kept = pl.ds(pl.multiple_of(core * hr + z * zr + yl * hz, hz), hz)
    given = pl.ds(pl.multiple_of(core * hr + z * zr + (1 - yl) * hz, hz), hz)
    lf[kept, :] = (lz[pl.ds(pl.multiple_of(yl * hz, hz), hz), :] + lr3[...]).astype(BF16)
    a6 = send(lf.at[kept], lf.at[kept], m2)
    t2.append(send(s2.at[hi], r2.at[hi], m2))
    fourth(2)
    wl[3].wait()
    pass_on(0)
    chain(0)
    chain(1)
    onward(2)
    fourth(3)
    multiply(0, True)
    pass_on(1)
    recv(a6, lf.at[given])
    a4 = {}
    for v, peer in hops:
        a4[v] = send(lf.at[piece], lf.at[piece], peer)
    multiply(3, False)
    multiply(1, False)
    away = pl.ds(pl.multiple_of((1 - yh) * qw, qw), qw)
    home = pl.ds(pl.multiple_of(yh * qw, qw), qw)
    py = {}

    def close(s, g):
        product(2, g, False)(s, 0)
        ps[s, :, side[g]] = acc[s, away, side[g]].astype(BF16)
        py[s, g] = send(ps.at[s, :, side[g]], pr.at[s, :, side[g]], yy)

    for s in (1, 2):
        recv(tm[s, 2], tx.at[s, 2])
    for g in range(2):
        recv(xf[0, g], cx.at[2, lo, side[g]])
        recv(xf[1, g], cx.at[2, hi, side[g]])
        for s in range(4):
            close(s, g)
    for v, peer in hops:
        recv(a4[v], lf.at[pl.ds(pl.multiple_of(core * hr + along(v) * zr, zr), zr)])
    a5 = send(lf.at[mine], lf.at[mine], m1)
    recv(tm[4, 2], tx.at[4, 2])
    close(4, 0)
    close(4, 1)
    recv(a5, lf.at[other])
    ex = {}
    for rel in (1, 3, 2, 0):
        q = lax.rem(x + rel, 4)
        gu = dot_tn(tq[q], lf[:, rank:2 * rank])
        ga = dot_tn(lf[:, 0:rank], cx[0, :, pl.ds(pl.multiple_of(q * qw, qw), qw)])
        gc = dot_tn(lf[:, 0:rank], cx[0, :, pl.ds(pl.multiple_of(4 * qw + q * qw, qw), qw)])
        if rel == 0:
            eo[0:2 * qw, :] = gu
            eo[2 * qw:2 * qw + rank, 0:qw] = ga
            eo[2 * qw:2 * qw + rank, qw:2 * qw] = gc
        else:
            eb[rel - 1, 0:2 * qw, :] = gu.astype(BF16)
            eb[rel - 1, 2 * qw:2 * qw + rank, 0:qw] = ga.astype(BF16)
            eb[rel - 1, 2 * qw:2 * qw + rank, qw:2 * qw] = gc.astype(BF16)
            ex[rel] = send(eb.at[rel - 1], er.at[rel - 1], px(rel))

    chain(2)
    chain(3)
    for rel in (1, 3, 2):
        recv(ex[rel], er.at[rel - 1])
        eo[...] = eo[...] + er[rel - 1].astype(F32)
    su[...] = eo[away, :].astype(BF16)
    sv[...] = eo[pl.ds(2 * qw, rank), away].astype(BF16)
    eu = send(su, eyu, yy)
    ev = send(sv, eyv, yy)

    recv(t1, r1)
    recv(t2[0], r2.at[lo])
    recv(t2[1], r2.at[hi])
    for c in range(CHUNKS):
        recv(t34[c], r34.at[pl.ds(c * cr, cr)])
    wl[0].wait()

    def total(n, carry):
        cols = pl.ds(pl.multiple_of(n * tile, tile), tile)
        value = dot_nt(cx[0], w[0, cols, :])
        value = value + dot_nt(lf[:, rank:2 * rank], uu[cols, :])
        value = value + r1[:, cols].astype(F32)
        value = value + r2[:, cols].astype(F32)
        gt[:, cols] = value + r34[:, cols].astype(F32)
        return carry

    lax.fori_loop(0, 4, total, 0)
    outs = [load(gt, gt_hbm)]
    for s in range(5):
        for g in range(2):
            recv(py[s, g], pr.at[s, :, side[g]])
        value = (acc[s, home, :] + pr[s].astype(F32)) * scale
        gb[s] = value.reshape(qw, 1, blk)
        outs.append(load(gb.at[s], gb_hbm.at[:, s]))
    recv(eu, eyu)
    recv(ev, eyv)
    gu_ref[...] = (eo[home, :] + eyu[...].astype(F32)) * scale
    gv_ref[...] = (eo[pl.ds(2 * qw, rank), home] + eyv[...].astype(F32)) * scale
    for cp in sent:
        cp.wait_send()
    for cp in outs:
        cp.wait()


def per_device(tokens, cotangent, blocks_w, lowrank_u, lowrank_v):
    rows, blk = tokens.shape
    rank = lowrank_u.shape[1]
    slots = blocks_w.shape[1]
    qw = blk // 8
    scale = 1.0 / math.sqrt(rows * lax.axis_size("dp"))
    big = (rows, blk)
    hr = rows // 2
    n_send = 64
    scratch = [
        pltpu.VMEM((4, rows, 2 * qw), BF16),
        pltpu.VMEM((4,) + big, BF16),
        pltpu.VMEM((slots, 4, rows, 2 * qw), BF16),
        pltpu.VMEM((slots, blk, blk), BF16),
        pltpu.VMEM((blk, rank), BF16),
        pltpu.VMEM((rank, blk), BF16),
    ]
    scratch += [pltpu.VMEM(big, BF16)] * 8
    scratch += [
        pltpu.VMEM((slots, 2 * qw, blk), F32),
        pltpu.VMEM((slots, qw, blk), BF16),
        pltpu.VMEM((slots, qw, blk), BF16),
        pltpu.VMEM(big, F32),
        pltpu.VMEM((slots, qw, 1, blk), F32),
        pltpu.VMEM((rows, 2 * rank), F32),
        pltpu.VMEM((hr, 2 * rank), F32),
        pltpu.VMEM((3, hr // 4, 2 * rank), F32),
        pltpu.VMEM((hr // 4, 2 * rank), F32),
        pltpu.VMEM((hr // 8, 2 * rank), F32),
        pltpu.VMEM((rows, 2 * rank), BF16),
        pltpu.VMEM((3, 2 * qw + rank, rank), BF16),
        pltpu.VMEM((3, 2 * qw + rank, rank), BF16),
        pltpu.VMEM((2 * qw + rank, rank), F32),
        pltpu.VMEM((qw, rank), BF16),
        pltpu.VMEM((rank, qw), BF16),
        pltpu.VMEM((qw, rank), BF16),
        pltpu.VMEM((rank, qw), BF16),
        pltpu.SemaphoreType.DMA((32,)),
        pltpu.SemaphoreType.DMA((n_send,)),
        pltpu.SemaphoreType.DMA((n_send,)),
    ]
    anyspace = pl.BlockSpec(memory_space=pl.ANY)
    vmem = pl.BlockSpec(memory_space=pltpu.VMEM)
    gt, gb, gu, gv = pl.pallas_call(
        functools.partial(kernel, rows, blk, rank, scale),
        out_shape=(
            jax.ShapeDtypeStruct(big, F32),
            jax.ShapeDtypeStruct((qw, slots, 1, blk), F32),
            jax.ShapeDtypeStruct((qw, rank), F32),
            jax.ShapeDtypeStruct((rank, qw), F32),
        ),
        in_specs=[anyspace] * 5,
        out_specs=(anyspace, anyspace, vmem, vmem),
        scratch_shapes=scratch,
        compiler_params=pltpu.CompilerParams(
            collective_id=0, has_side_effects=True, vmem_limit_bytes=64 << 20
        ),
        name="butterfly",
    )(tokens, cotangent, blocks_w[0], lowrank_u, lowrank_v)
    return gt, jnp.transpose(gb, (0, 2, 1, 3)), gu, gv


def solution(mesh):
    in_specs = (
        P("dp", "mp"),
        P("dp", "mp"),
        P("mp", None, None, None),
        P("mp", None),
        P(None, "mp"),
    )
    out_specs = (
        P("dp", "mp"),
        P("dp", "mp", None, None),
        P(("mp", "dp"), None),
        P(None, ("mp", "dp")),
    )
    return jax.shard_map(
        per_device, mesh=mesh, in_specs=in_specs, out_specs=out_specs, check_vma=False
    )
```
